32 devices in a mesh: wide: 8 (over y, x, core), blk: 4 (over z).
Axes of the slice: x: 2, y: 2, z: 4, core: 2. Of those that a mesh axis runs over, the one named last changes fastest.
Arguments:
- sources: bfloat16 [32, 64000], P(('wide', 'blk')), may hold values from -6 to 6
- targets: bfloat16 [4, 64000], P('blk'), may hold values from -6 to 6
Outputs:
- exchange_field: float32 [4, 64000], P('blk', 'wide')
The draws below stay inside these ranges and needn't reach their ends.
All inputs are finite; a program needn't handle non-finite values.
Results may differ from the reference program's by a relative error of at most 0.014.
Values may be sent and summed in bfloat16 or wider, within the bound.
A program may use at most 64 MiB of HBM per device.

```python
import math
import jax
import jax.numpy as jnp
from jax import lax

GRID = 40
SRC_DEV = 1
HOPS = 2
CELLS = 64000
SOURCES = 32
TARGETS = 4
N_WIDE = 8
N_BLK = 4


def spiked(drawn, stream_key, source, target, shards_of, factor):
    owner, partner = [(jnp.arange(drawn.shape[axis_at]) // (drawn.shape[axis_at] // shards_of)).reshape([-1 if axis == axis_at else 1 for axis in range(drawn.ndim)]) for axis_at in (source, target)]
    chosen = jax.random.permutation(stream_key, shards_of)[partner]
    strong = (owner == chosen) | (owner == (partner + shards_of // 2) % shards_of)
    return jnp.where(strong, factor * drawn, drawn)


def level_of(key, dims, shards, low, top_value):
    level = 1.0
    for axis_at, blocks in shards:
        steps = jax.random.uniform(jax.random.fold_in(jax.random.fold_in(key, 6), axis_at), (blocks,), jnp.float32, low / len(shards), top_value / len(shards))
        level = level * jnp.repeat(jnp.exp(steps), dims[axis_at] // blocks).reshape((-1,) + (1,) * (len(dims) - 1 - axis_at))
    return level


def scatter_about(key, shape, spread, most, shards=(), kind=jnp.bfloat16):
    loudness = level_of(key, shape, shards, -0.22, 0.18) if shards else 1.0
    entries = jax.random.normal(key, shape, jnp.float32) * spread * loudness
    return jnp.minimum(jnp.maximum(entries, -most), most).astype(kind)


def noise_with(key, shape, scale, limit, cuts, heavy, kind=jnp.bfloat16):
    entries = scale * jax.random.normal(key, shape, jnp.float32)
    if cuts:
        entries = entries * level_of(key, shape, cuts, -0.22, 0.18)
    return jnp.clip(spiked(entries, jax.random.fold_in(key, 3), *heavy), -limit, limit).astype(kind)


def setup_inputs(seed: int = 0) -> dict:
    key_of = jax.random.split(jax.random.key(seed), 3)
    sources = noise_with(key_of[0], (SOURCES, CELLS), (HOPS * N_WIDE // 4) ** -0.5, 6.0, ((0, 32),), (0, 1, 32, 2.75))
    targets = scatter_about(key_of[1], (TARGETS, CELLS), 1.0, 6.0, ((0, 4),))
    return {"sources": sources, "targets": targets}


screen = 0.3


def tables(grid):
    index = jnp.arange(grid, dtype=jnp.int32)
    product = (index[:, None] * index[None, :]) % grid
    angle = (2.0 * math.pi / grid) * product.astype(jnp.float32)
    return jnp.concatenate([jnp.cos(angle), jnp.sin(angle)], axis=0).astype(jnp.bfloat16)


def kernel_table(grid):
    index = jnp.arange(grid, dtype=jnp.int32)
    wrapped = ((index + grid // 2) % grid) - grid // 2
    wave = (2.0 * math.pi / grid) * wrapped.astype(jnp.float32)
    square = wave * wave
    total = square[:, None, None] + square[None, :, None] + square[None, None, :]
    values = (4.0 * math.pi) / (total + screen * screen) / float(grid ** 3)
    return values.reshape(grid, grid * grid)


def turn(field, both):
    width = both.shape[1]
    cos_table = both[:width].astype(jnp.float32)
    sin_table = both[width:].astype(jnp.float32)
    wide_field = field.astype(jnp.float32)
    cpart = jnp.einsum("mnr,kn->mrk", wide_field, cos_table, precision=lax.Precision.HIGHEST)
    spart = jnp.einsum("mnr,kn->mrk", wide_field, sin_table, precision=lax.Precision.HIGHEST)
    return cpart.reshape(field.shape), spart.reshape(field.shape)


def potential(pair, both, kern):
    cpart, spart = turn(pair, both)
    real_part = cpart.astype(jnp.bfloat16)
    imag_part = (-spart).astype(jnp.bfloat16)
    for section in range(2):
        rcos, rsin = turn(real_part, both)
        icos, isin = turn(imag_part, both)
        new_real = rcos + isin
        new_imag = icos - rsin
        if section == 1:
            new_real = new_real * kern
            new_imag = new_imag * kern
        real_part = new_real.astype(jnp.bfloat16)
        imag_part = new_imag.astype(jnp.bfloat16)
    for section in range(2):
        rcos, rsin = turn(real_part, both)
        icos, isin = turn(imag_part, both)
        real_part = (rcos - isin).astype(jnp.bfloat16)
        imag_part = (icos + rsin).astype(jnp.bfloat16)
    rcos, rsin = turn(real_part, both)
    icos, isin = turn(imag_part, both)
    return rcos - isin


def exchange_term(chosen, target, both, kern):
    grid = both.shape[1]
    count = chosen.shape[0]
    pair = (chosen.astype(jnp.float32) * target.astype(jnp.float32)[None, :]).astype(jnp.bfloat16)
    pair = pair.reshape(count, grid, grid * grid)
    field = potential(pair, both, kern).reshape(count, grid ** 3)
    return -jnp.sum(chosen.astype(jnp.float32) * field, axis=0)


def reference(sources, targets):
    both = tables(GRID)
    kern = kernel_table(GRID)
    blocks = sources.reshape(N_WIDE, N_BLK, SRC_DEV, CELLS)

    def one_row(row):
        owner = ((row - HOPS + 1) % N_BLK).astype(jnp.int32)
        picks = ((owner + jnp.arange(HOPS, dtype=jnp.int32)) % N_BLK).astype(jnp.int32)
        chosen = jnp.take(blocks, picks, axis=1).reshape(N_WIDE * HOPS * SRC_DEV, CELLS)
        target = lax.dynamic_index_in_dim(targets, owner, 0, keepdims=False)
        return exchange_term(chosen, target, both, kern)

    return lax.map(one_row, jnp.arange(N_BLK, dtype=jnp.int32))
```

```python
import functools
import math

import jax
import jax.numpy as jnp
import numpy as np
from jax import lax
from jax.experimental import pallas as pl
from jax.experimental.pallas import tpu as pltpu
from jax.sharding import PartitionSpec as P

MESH = pl.DeviceIdType.MESH
LANES = 128
SCREEN = 0.3
F32 = jnp.float32
BF16 = jnp.bfloat16


def basis(grid):
    half = grid // 2
    index = np.arange(grid)
    angle = 2.0 * math.pi / grid * ((index[:, None] * index[None, :]) % grid)
    cosines = np.cos(angle).astype(np.float32).astype(BF16).astype(np.float32)
    sines = np.sin(angle).astype(np.float32).astype(BF16).astype(np.float32)
    odd = np.arange(1, (grid + 1) // 2)
    q = np.concatenate([cosines[: half + 1], sines[odd]], axis=0)
    freq = np.concatenate([index[: half + 1], odd])
    weight = np.where(np.isin(freq, odd), 2.0, 1.0)
    return q, freq, weight


def plan(grid):
    q, freq, weight = basis(grid)
    group = max(d for d in range(1, grid + 1) if grid % d == 0 and d * grid <= 2 * LANES)
    per = grid // group
    wide = 2 * LANES
    a_mat = np.kron(q, np.eye(per))
    b_mat = np.kron(np.eye(group), q)
    c_mat = np.zeros((2, wide, group, LANES), np.float32)
    for h in range(2):
        lane = h * (LANES // 2)
        for j in range(group):
            c_mat[h, j * grid : (j + 1) * grid, j, lane : lane + grid] = q.T
    c_mat = c_mat.reshape(2 * wide, group * LANES)
    wave = 2.0 * math.pi / grid * freq
    sq = wave * wave
    total = sq[:, None, None] + sq[None, :, None] + sq[None, None, :]
    kern = 4.0 * math.pi / (total + SCREEN * SCREEN) / float(grid**3)
    kern = kern * weight[:, None, None] * weight[None, :, None] * weight[None, None, :]
    packed = np.zeros((grid // 2, grid, 2, LANES // 2), np.float32)
    for h in range(2):
        packed[:, :, h, :grid] = kern[h * (grid // 2) : (h + 1) * (grid // 2)]
    packed = packed.reshape(grid // 2 * grid, LANES)
    mats = [a_mat, a_mat.T, b_mat, b_mat.T, c_mat, c_mat.T]
    return group, [m.astype(BF16) for m in mats] + [packed.astype(np.float32)]


def dot(x, y):
    return jnp.dot(x, y, preferred_element_type=F32)


def exchange(pair, tables, y_ref, grid, group):
    a_ref, at_ref, b_ref, bt_ref, c_ref, ct_ref, k_ref = tables
    rows, wide = pair.shape
    hrows = rows // 2
    z = dot(a_ref[...], pair).astype(BF16)
    z = jnp.concatenate([z[:hrows], z[hrows:]], axis=1)
    y = dot(z, c_ref[...])
    for j in range(group):
        y_ref[pl.ds(j, hrows, stride=group), :] = y[:, j * LANES : (j + 1) * LANES]
    block = group * grid
    chunks = y_ref.shape[0] // block
    for i in range(0, chunks, 2):
        spans = [pl.ds(k * block, block) for k in (i, i + 1)]
        x = jnp.concatenate([y_ref[s, :].astype(BF16) for s in spans], axis=1)
        kern = jnp.concatenate([k_ref[s, :] for s in spans], axis=1)
        spec = (dot(b_ref[...], x) * kern).astype(BF16)
        back = dot(bt_ref[...], spec)
        for n, s in enumerate(spans):
            y_ref[s, :] = back[:, n * LANES : (n + 1) * LANES]
    x = jnp.concatenate(
        [y_ref[pl.ds(j, hrows, stride=group), :].astype(BF16) for j in range(group)], axis=1
    )
    z = dot(x, ct_ref[...]).astype(BF16)
    z = jnp.concatenate([z[:, :wide], z[:, wide:]], axis=0)
    return dot(at_ref[...], z)


def kernel(n_wide, n_blk, grid, group, src_ref, tgt_ref, *rest):
    tables = rest[:7]
    out_ref = rest[7]
    (y_ref, tgt_next, first_out, first_in, total, parts_out, parts_in,
     send_sem, recv_sem) = rest[8:]
    w = lax.axis_index("wide")
    b = lax.axis_index("blk")
    ahead = (w, lax.rem(b + 1, n_blk))
    behind = (w, lax.rem(b + n_blk - 1, n_blk))
    peers = [(lax.rem(w + d, n_wide), b) for d in range(1, n_wide)]
    barrier = pltpu.get_barrier_semaphore()
    greeted = [ahead, behind] + peers
    for device in greeted:
        pl.semaphore_signal(barrier, inc=1, device_id=device, device_id_type=MESH)
    pl.semaphore_wait(barrier, len(greeted))

    def send(src, dst, slot, device):
        copy = pltpu.make_async_remote_copy(
            src_ref=src, dst_ref=dst, send_sem=send_sem.at[slot], recv_sem=recv_sem.at[slot],
            device_id=device, device_id_type=MESH,
        )
        copy.start()
        return copy

    target_copy = send(tgt_ref, tgt_next, 0, ahead)
    source = src_ref[...].astype(F32)
    pair = (source * tgt_ref[...].astype(F32)).astype(BF16)
    term = source * exchange(pair, tables, y_ref, grid, group)
    first_out[...] = term.astype(BF16)
    first_copy = send(first_out, first_in, 1, ahead)
    target_copy.wait()
    source = src_ref[...].astype(F32)
    pair = (source * tgt_next[...].astype(F32)).astype(BF16)
    term = source * exchange(pair, tables, y_ref, grid, group)
    first_copy.wait()
    term = -(term + first_in[...].astype(F32))
    rows = term.shape[0] // n_wide
    for k in range(n_wide):
        piece = term[k * rows : (k + 1) * rows]
        total[k] = piece
        parts_out[k] = piece.astype(BF16)
    copies = [
        send(parts_out.at[peers[d][0]], parts_in.at[d], 2 + d, peers[d]) for d in range(n_wide - 1)
    ]
    summed = total[w]
    for d, copy in enumerate(copies):
        copy.wait()
        summed = summed + parts_in[d].astype(F32)
    out_ref[...] = summed


def shards(n_wide, n_blk, sources, targets):
    cells = sources.shape[1]
    grid = round(cells ** (1.0 / 3.0))
    group, tables = plan(grid)
    wide = 2 * LANES
    rows = cells // (group * grid)

    def laid(x):
        x = x.reshape(rows, group * grid)
        return jnp.pad(x, ((0, 0), (0, wide - group * grid)))

    part = rows // n_wide
    vmem = pl.BlockSpec(memory_space=pltpu.VMEM)
    result = pl.pallas_call(
        functools.partial(kernel, n_wide, n_blk, grid, group),
        out_shape=jax.ShapeDtypeStruct((part, wide), F32),
        in_specs=[vmem] * 9,
        out_specs=vmem,
        scratch_shapes=[
            pltpu.VMEM((rows // 2 * group, LANES), F32),
            pltpu.VMEM((rows, wide), BF16),
            pltpu.VMEM((rows, wide), BF16),
            pltpu.VMEM((rows, wide), BF16),
            pltpu.VMEM((n_wide, part, wide), F32),
            pltpu.VMEM((n_wide, part, wide), BF16),
            pltpu.VMEM((n_wide - 1, part, wide), BF16),
            pltpu.SemaphoreType.DMA((n_wide + 1,)),
            pltpu.SemaphoreType.DMA((n_wide + 1,)),
        ],
        compiler_params=pltpu.CompilerParams(collective_id=0, has_side_effects=True),
    )(laid(sources), laid(targets), *[jnp.asarray(t) for t in tables])
    return result[:, : group * grid].reshape(1, cells // n_wide)


def solution(mesh):
    body = functools.partial(shards, mesh.shape["wide"], mesh.shape["blk"])
    in_specs = (P(("wide", "blk"), None), P("blk", None))
    return jax.shard_map(
        body, mesh=mesh, in_specs=in_specs, out_specs=P("blk", "wide"), check_vma=False
    )
```

```python
import functools
import math

import jax
import jax.numpy as jnp
import numpy as np
from jax import lax
from jax.experimental import pallas as pl
from jax.experimental.pallas import tpu as pltpu
from jax.sharding import PartitionSpec as P

MESH = pl.DeviceIdType.MESH
LANES = 128
SCREEN = 0.3
F32 = jnp.float32
BF16 = jnp.bfloat16


def basis(grid):
    half = grid // 2
    index = np.arange(grid)
    angle = 2.0 * math.pi / grid * ((index[:, None] * index[None, :]) % grid)
    cosines = np.cos(angle).astype(np.float32).astype(BF16).astype(np.float32)
    sines = np.sin(angle).astype(np.float32).astype(BF16).astype(np.float32)
    odd = np.arange(1, (grid + 1) // 2)
    q = np.concatenate([cosines[: half + 1], sines[odd]], axis=0)
    freq = np.concatenate([index[: half + 1], odd])
    weight = np.where(np.isin(freq, odd), 2.0, 1.0)
    return q, freq, weight


def plan(grid):
    q, freq, weight = basis(grid)
    group = max(d for d in range(1, grid + 1) if grid % d == 0 and d * grid <= 2 * LANES)
    per = grid // group
    wide = 2 * LANES
    a_mat = np.kron(q, np.eye(per))
    b_mat = np.kron(np.eye(group), q)
    c_mat = np.zeros((2, wide, group, LANES), np.float32)
    for h in range(2):
        lane = h * (LANES // 2)
        for j in range(group):
            c_mat[h, j * grid : (j + 1) * grid, j, lane : lane + grid] = q.T
    c_mat = c_mat.reshape(2 * wide, group * LANES)
    wave = 2.0 * math.pi / grid * freq
    sq = wave * wave
    total = sq[:, None, None] + sq[None, :, None] + sq[None, None, :]
    kern = 4.0 * math.pi / (total + SCREEN * SCREEN) / float(grid**3)
    kern = kern * weight[:, None, None] * weight[None, :, None] * weight[None, None, :]
    packed = np.zeros((grid // 2, grid, 2, LANES // 2), np.float32)
    for h in range(2):
        packed[:, :, h, :grid] = kern[h * (grid // 2) : (h + 1) * (grid // 2)]
    packed = packed.reshape(grid // 2 * grid, LANES)
    mats = [a_mat, a_mat.T, b_mat, b_mat.T, c_mat, c_mat.T]
    return group, [m.astype(BF16) for m in mats] + [packed.astype(np.float32)]


def dot(x, y):
    return jnp.dot(x, y, preferred_element_type=F32)


def exchange(pair, tables, y_ref, grid, group):
    a_ref, at_ref, b_ref, bt_ref, c_ref, ct_ref, k_ref = tables
    rows, wide = pair.shape
    hrows = rows // 2
    z = dot(a_ref[...], pair).astype(BF16)
    z = jnp.concatenate([z[:hrows], z[hrows:]], axis=1)
    y = dot(z, c_ref[...])
    for j in range(group):
        y_ref[pl.ds(j, hrows, stride=group), :] = y[:, j * LANES : (j + 1) * LANES]
    block = group * grid
    chunks = y_ref.shape[0] // block
    for i in range(0, chunks, 2):
        spans = [pl.ds(k * block, block) for k in (i, i + 1)]
        x = jnp.concatenate([y_ref[s, :].astype(BF16) for s in spans], axis=1)
        kern = jnp.concatenate([k_ref[s, :] for s in spans], axis=1)
        spec = (dot(b_ref[...], x) * kern).astype(BF16)
        back = dot(bt_ref[...], spec)
        for n, s in enumerate(spans):
            y_ref[s, :] = back[:, n * LANES : (n + 1) * LANES]
    x = jnp.concatenate(
        [y_ref[pl.ds(j, hrows, stride=group), :].astype(BF16) for j in range(group)], axis=1
    )
    z = dot(x, ct_ref[...]).astype(BF16)
    z = jnp.concatenate([z[:, :wide], z[:, wide:]], axis=0)
    return dot(at_ref[...], z)


def relaid(raw_ref, flat_ref, z_ref, width):
    flat_ref[...] = raw_ref[...].astype(F32).reshape(flat_ref.shape)
    period = math.lcm(width, LANES)
    tiles = period // LANES
    lines = period // width
    count = flat_ref.shape[0] // tiles
    columns = [flat_ref[pl.ds(t, count, stride=tiles), :] for t in range(tiles)]
    lane = lax.broadcasted_iota(jnp.int32, (count, LANES), 1)
    for j in range(lines):
        first, shift = divmod(width * j, LANES)
        need = max(2, -(-(shift + width) // LANES))
        x = jnp.concatenate(columns[first : first + need], axis=1)
        if shift:
            x = pltpu.roll(x, need * LANES - shift, 1)
        for half in range(2):
            piece = x[:, half * LANES : (half + 1) * LANES]
            piece = jnp.where(lane + half * LANES < width, piece, 0.0)
            z_ref[half, pl.ds(j, count, stride=lines), :] = piece
    return jnp.concatenate([z_ref[0], z_ref[1]], axis=1)


def kernel(n_wide, n_blk, grid, group, src_ref, tgt_ref, *rest):
    table_hbm = rest[:7]
    out_ref = rest[7]
    tables = rest[8:15]
    (y_ref, flat_ref, z_ref, source_ref, tgt_out, tgt_in, total, parts_out, parts_in,
     passed_out, passed_in, table_sem, send_sem, recv_sem) = rest[15:]
    w = lax.axis_index("wide")
    b = lax.axis_index("blk")
    width = group * grid
    loads = [
        pltpu.make_async_copy(hbm, ref, table_sem.at[i])
        for i, (hbm, ref) in enumerate(zip(table_hbm, tables))
    ]
    for load in loads:
        load.start()
    core = lax.rem(w, 2)
    ahead = (w, lax.rem(b + 1, n_blk))
    behind = (w, lax.rem(b + n_blk - 1, n_blk))
    partner = (w + 1 - 2 * core, b)
    peers = [(lax.rem(w + d, n_wide), b) for d in range(1, n_wide)]
    barrier = pltpu.get_barrier_semaphore()
    greeted = [ahead, behind] + peers
    for device in greeted:
        pl.semaphore_signal(barrier, inc=1, device_id=device, device_id_type=MESH)

    def send(src, dst, slot, device):
        copy = pltpu.make_async_remote_copy(
            src_ref=src, dst_ref=dst, send_sem=send_sem.at[slot], recv_sem=recv_sem.at[slot],
            device_id=device, device_id_type=MESH,
        )
        copy.start()
        return copy

    target = relaid(tgt_ref, flat_ref, z_ref, width)
    tgt_out[...] = target.reshape(tgt_out.shape).astype(BF16)
    quarter = tgt_out.shape[0] // 2
    pl.semaphore_wait(barrier, len(greeted))
    hops = [
        send(tgt_out.at[core * quarter + k], tgt_in.at[core * quarter + k], k, ahead)
        for k in range(quarter)
    ]
    source = relaid(src_ref, flat_ref, z_ref, width)
    source_ref[...] = source
    for load in loads:
        load.wait()
    rows = source.shape[0] // n_wide

    def scatter(target, turn):
        pair = (source_ref[...] * target).astype(BF16)
        term = source_ref[...] * exchange(pair, tables, y_ref, grid, group)
        for k in range(n_wide):
            piece = term[k * rows : (k + 1) * rows]
            total[turn, k] = piece
            parts_out[turn, k] = piece.astype(BF16)
        slot = 2 * quarter + 1 + turn * (n_wide - 1)
        return [
            send(parts_out.at[turn, peers[d][0]], parts_in.at[turn, d], slot + d, peers[d])
            for d in range(n_wide - 1)
        ]

    def gathered(copies, turn):
        summed = total[turn, w]
        for d, copy in enumerate(copies):
            copy.wait()
            summed = summed + parts_in[turn, d].astype(F32)
        return summed

    first = scatter(target, 0)
    relays = []
    for k, hop in enumerate(hops):
        hop.wait()
        here = tgt_in.at[core * quarter + k]
        relays.append(send(here, here, quarter + k, partner))
    passed_out[...] = gathered(first, 0).astype(BF16)
    passed = send(passed_out, passed_in, 2 * quarter, ahead)
    for relay in relays:
        relay.wait()
    second = scatter(tgt_in[...].astype(F32).reshape(source.shape), 1)
    passed.wait()
    summed = -(gathered(second, 1) + passed_in[...].astype(F32))
    for k in range(rows):
        out_ref[0:1, k * width : (k + 1) * width] = summed[k : k + 1, :width]


def shards(n_wide, n_blk, sources, targets):
    cells = sources.shape[1]
    grid = round(cells ** (1.0 / 3.0))
    group, tables = plan(grid)
    wide = 2 * LANES
    rows = cells // (group * grid)
    part = rows // n_wide
    line = 8 * (rows // 64)
    vmem = pl.BlockSpec(memory_space=pltpu.VMEM)
    hbm = pl.BlockSpec(memory_space=pl.ANY)
    sems = 2 * (rows // line // 2) + 1 + 2 * (n_wide - 1)
    return pl.pallas_call(
        functools.partial(kernel, n_wide, n_blk, grid, group),
        out_shape=jax.ShapeDtypeStruct((1, cells // n_wide), F32),
        in_specs=[vmem] * 2 + [hbm] * 7,
        out_specs=vmem,
        scratch_shapes=[pltpu.VMEM(t.shape, t.dtype) for t in tables]
        + [
            pltpu.VMEM((rows // 2 * group, LANES), F32),
            pltpu.VMEM((cells // LANES, LANES), F32),
            pltpu.VMEM((2, rows, LANES), F32),
            pltpu.VMEM((rows, wide), F32),
            pltpu.VMEM((rows // line, line, wide), BF16),
            pltpu.VMEM((rows // line, line, wide), BF16),
            pltpu.VMEM((2, n_wide, part, wide), F32),
            pltpu.VMEM((2, n_wide, part, wide), BF16),
            pltpu.VMEM((2, n_wide - 1, part, wide), BF16),
            pltpu.VMEM((part, wide), BF16),
            pltpu.VMEM((part, wide), BF16),
            pltpu.SemaphoreType.DMA((len(tables),)),
            pltpu.SemaphoreType.DMA((sems,)),
            pltpu.SemaphoreType.DMA((sems,)),
        ],
        compiler_params=pltpu.CompilerParams(collective_id=0, has_side_effects=True),
    )(sources, targets, *[jnp.asarray(t) for t in tables])


def solution(mesh):
    body = functools.partial(shards, mesh.shape["wide"], mesh.shape["blk"])
    in_specs = (P(("wide", "blk"), None), P("blk", None))
    return jax.shard_map(
        body, mesh=mesh, in_specs=in_specs, out_specs=P("blk", "wide"), check_vma=False
    )
```

```python
import functools
import math

import jax
import jax.numpy as jnp
import numpy as np
from jax import lax
from jax.experimental import pallas as pl
from jax.experimental.pallas import tpu as pltpu
from jax.sharding import PartitionSpec as P

MESH = pl.DeviceIdType.MESH
LANES = 128
SCREEN = 0.3
F32 = jnp.float32
BF16 = jnp.bfloat16


def basis(grid):
    half = grid // 2
    index = np.arange(grid)
    angle = 2.0 * math.pi / grid * ((index[:, None] * index[None, :]) % grid)
    cosines = np.cos(angle).astype(np.float32).astype(BF16).astype(np.float32)
    sines = np.sin(angle).astype(np.float32).astype(BF16).astype(np.float32)
    odd = np.arange(1, (grid + 1) // 2)
    q = np.concatenate([cosines[: half + 1], sines[odd]], axis=0)
    freq = np.concatenate([index[: half + 1], odd])
    weight = np.where(np.isin(freq, odd), 2.0, 1.0)
    return q, freq, weight


def plan(grid):
    q, freq, weight = basis(grid)
    group = max(d for d in range(1, grid + 1) if grid % d == 0 and d * grid <= 2 * LANES)
    per = grid // group
    wide = 2 * LANES
    a_mat = np.kron(q, np.eye(per))
    b_mat = np.kron(np.eye(group), q)
    c_mat = np.zeros((2, wide, group, LANES), np.float32)
    for h in range(2):
        lane = h * (LANES // 2)
        for j in range(group):
            c_mat[h, j * grid : (j + 1) * grid, j, lane : lane + grid] = q.T
    c_mat = c_mat.reshape(2 * wide, group * LANES)
    wave = 2.0 * math.pi / grid * freq
    sq = wave * wave
    total = sq[:, None, None] + sq[None, :, None] + sq[None, None, :]
    kern = 4.0 * math.pi / (total + SCREEN * SCREEN) / float(grid**3)
    kern = kern * weight[:, None, None] * weight[None, :, None] * weight[None, None, :]
    packed = np.zeros((grid // 2, grid, 2, LANES // 2), np.float32)
    for h in range(2):
        packed[:, :, h, :grid] = kern[h * (grid // 2) : (h + 1) * (grid // 2)]
    packed = packed.reshape(grid // 2 * grid, LANES)
    mats = [a_mat, a_mat.T, b_mat, b_mat.T, c_mat, c_mat.T]
    return group, [m.astype(BF16) for m in mats] + [packed.astype(np.float32)]


def dot(x, y):
    return jnp.dot(x, y, preferred_element_type=F32)


def exchange(pair, tables, y_ref, grid, group):
    a_ref, at_ref, b_ref, bt_ref, c_ref, ct_ref, k_ref = tables
    rows, wide = pair.shape
    hrows = rows // 2
    z = dot(a_ref[...], pair).astype(BF16)
    z = jnp.concatenate([z[:hrows], z[hrows:]], axis=1)
    y = dot(z, c_ref[...])
    for j in range(group):
        y_ref[pl.ds(j, hrows, stride=group), :] = y[:, j * LANES : (j + 1) * LANES]
    block = group * grid
    chunks = y_ref.shape[0] // block
    for i in range(0, chunks, 2):
        spans = [pl.ds(k * block, block) for k in (i, i + 1)]
        x = jnp.concatenate([y_ref[s, :].astype(BF16) for s in spans], axis=1)
        kern = jnp.concatenate([k_ref[s, :] for s in spans], axis=1)
        spec = (dot(b_ref[...], x) * kern).astype(BF16)
        back = dot(bt_ref[...], spec)
        for n, s in enumerate(spans):
            y_ref[s, :] = back[:, n * LANES : (n + 1) * LANES]
    x = jnp.concatenate(
        [y_ref[pl.ds(j, hrows, stride=group), :].astype(BF16) for j in range(group)], axis=1
    )
    z = dot(x, ct_ref[...]).astype(BF16)
    z = jnp.concatenate([z[:, :wide], z[:, wide:]], axis=0)
    return dot(at_ref[...], z)


def relaid(raw_ref, flat_ref, z_ref, width):
    flat_ref[...] = raw_ref[...].astype(F32).reshape(flat_ref.shape)
    period = math.lcm(width, LANES)
    tiles = period // LANES
    lines = period // width
    count = flat_ref.shape[0] // tiles
    columns = [flat_ref[pl.ds(t, count, stride=tiles), :] for t in range(tiles)]
    lane = lax.broadcasted_iota(jnp.int32, (count, LANES), 1)
    for j in range(lines):
        first, shift = divmod(width * j, LANES)
        need = max(2, -(-(shift + width) // LANES))
        x = jnp.concatenate(columns[first : first + need], axis=1)
        if shift:
            x = pltpu.roll(x, need * LANES - shift, 1)
        for half in range(2):
            piece = x[:, half * LANES : (half + 1) * LANES]
            piece = jnp.where(lane + half * LANES < width, piece, 0.0)
            z_ref[half, pl.ds(j, count, stride=lines), :] = piece
    return jnp.concatenate([z_ref[0], z_ref[1]], axis=1)


def partners(w, n_wide):
    if n_wide & (n_wide - 1):
        return [(lax.rem(w + d, n_wide), d - 1) for d in range(1, n_wide)]
    bits = [1 << k for k in range(n_wide.bit_length() - 1)]
    found = []
    for d in range(1, n_wide):
        flips = [bit for bit in bits if d & bit]
        other = w
        for bit in flips:
            other = other + bit - 2 * bit * lax.rem(w // bit, 2)
        found.append((len([bit for bit in flips if bit > 1]), d, other))
    found.sort(key=lambda item: (-item[0], item[1]))
    return [(other, d - 1) for _, d, other in found]


def kernel(n_wide, n_blk, grid, group, src_hbm, tgt_hbm, *rest):
    table_hbm = rest[:7]
    out_ref = rest[7]
    tables = rest[8:15]
    (src_ref, tgt_ref, y_ref, flat_ref, z_ref, source_ref, tgt_out, tgt_in, total, parts_out, parts_in,
     passed_out, passed_in, raw_sem, table_sem, send_sem, recv_sem) = rest[15:]
    w = lax.axis_index("wide")
    b = lax.axis_index("blk")
    width = group * grid
    raw = [
        pltpu.make_async_copy(hbm, ref, raw_sem.at[i])
        for i, (hbm, ref) in enumerate(((tgt_hbm, tgt_ref), (src_hbm, src_ref)))
    ]
    for load in raw:
        load.start()
    loads = [
        pltpu.make_async_copy(hbm, ref, table_sem.at[i])
        for i, (hbm, ref) in enumerate(zip(table_hbm, tables))
    ]
    core = lax.rem(w, 2)
    ahead = (w, lax.rem(b + 1, n_blk))
    behind = (w, lax.rem(b + n_blk - 1, n_blk))
    partner = (w + 1 - 2 * core, b)
    peers = partners(w, n_wide)
    barrier = pltpu.get_barrier_semaphore()
    greeted = [ahead, behind] + [(other, b) for other, _ in peers]
    for device in greeted:
        pl.semaphore_signal(barrier, inc=1, device_id=device, device_id_type=MESH)

    def send(src, dst, slot, device):
        copy = pltpu.make_async_remote_copy(
            src_ref=src, dst_ref=dst, send_sem=send_sem.at[slot], recv_sem=recv_sem.at[slot],
            device_id=device, device_id_type=MESH,
        )
        copy.start()
        return copy

    for load in loads:
        load.start()
    raw[0].wait()
    target = relaid(tgt_ref, flat_ref, z_ref, width)
    tgt_out[...] = target.reshape(tgt_out.shape).astype(BF16)
    quarter = tgt_out.shape[0] // 2
    pl.semaphore_wait(barrier, len(greeted))
    hops = [
        send(tgt_out.at[core * quarter + k], tgt_in.at[core * quarter + k], k, ahead)
        for k in range(quarter)
    ]
    raw[1].wait()
    source = relaid(src_ref, flat_ref, z_ref, width)
    source_ref[...] = source
    for load in loads:
        load.wait()
    rows = source.shape[0] // n_wide

    def scatter(target, turn):
        pair = (source_ref[...] * target).astype(BF16)
        term = source_ref[...] * exchange(pair, tables, y_ref, grid, group)
        for k in range(n_wide):
            piece = term[k * rows : (k + 1) * rows]
            total[turn, k] = piece
            parts_out[turn, k] = piece.astype(BF16)
        slot = 2 * quarter + 1 + turn * (n_wide - 1)
        return [
            send(parts_out.at[turn, other], parts_in.at[turn, d], slot + d, (other, b))
            for other, d in peers
        ]

    def gathered(copies, turn):
        summed = total[turn, w]
        for (_, d), copy in reversed(list(zip(peers, copies))):
            copy.wait()
            summed = summed + parts_in[turn, d].astype(F32)
        return summed

    first = scatter(target, 0)
    relays = []
    for k, hop in enumerate(hops):
        hop.wait()
        here = tgt_in.at[core * quarter + k]
        relays.append(send(here, here, quarter + k, partner))
    for relay in relays:
        relay.wait()
    second = scatter(tgt_in[...].astype(F32).reshape(source.shape), 1)
    passed_out[...] = gathered(first, 0).astype(BF16)
    passed = send(passed_out, passed_in, 2 * quarter, ahead)
    summed = gathered(second, 1)
    passed.wait()
    summed = -(summed + passed_in[...].astype(F32))
    for k in range(rows):
        out_ref[0:1, k * width : (k + 1) * width] = summed[k : k + 1, :width]


def shards(n_wide, n_blk, sources, targets):
    cells = sources.shape[1]
    grid = round(cells ** (1.0 / 3.0))
    group, tables = plan(grid)
    wide = 2 * LANES
    rows = cells // (group * grid)
    part = rows // n_wide
    line = 8 * (rows // 64)
    vmem = pl.BlockSpec(memory_space=pltpu.VMEM)
    hbm = pl.BlockSpec(memory_space=pl.ANY)
    sems = 2 * (rows // line // 2) + 1 + 2 * (n_wide - 1)
    return pl.pallas_call(
        functools.partial(kernel, n_wide, n_blk, grid, group),
        out_shape=jax.ShapeDtypeStruct((1, cells // n_wide), F32),
        in_specs=[hbm] * 9,
        out_specs=vmem,
        scratch_shapes=[pltpu.VMEM(t.shape, t.dtype) for t in tables]
        + [
            pltpu.VMEM((1, cells), BF16),
            pltpu.VMEM((1, cells), BF16),
            pltpu.VMEM((rows // 2 * group, LANES), F32),
            pltpu.VMEM((cells // LANES, LANES), F32),
            pltpu.VMEM((2, rows, LANES), F32),
            pltpu.VMEM((rows, wide), F32),
            pltpu.VMEM((rows // line, line, wide), BF16),
            pltpu.VMEM((rows // line, line, wide), BF16),
            pltpu.VMEM((2, n_wide, part, wide), F32),
            pltpu.VMEM((2, n_wide, part, wide), BF16),
            pltpu.VMEM((2, n_wide - 1, part, wide), BF16),
            pltpu.VMEM((part, wide), BF16),
            pltpu.VMEM((part, wide), BF16),
            pltpu.SemaphoreType.DMA((2,)),
            pltpu.SemaphoreType.DMA((len(tables),)),
            pltpu.SemaphoreType.DMA((sems,)),
            pltpu.SemaphoreType.DMA((sems,)),
        ],
        compiler_params=pltpu.CompilerParams(collective_id=0, has_side_effects=True),
    )(sources, targets, *[jnp.asarray(t) for t in tables])


def solution(mesh):
    body = functools.partial(shards, mesh.shape["wide"], mesh.shape["blk"])
    in_specs = (P(("wide", "blk"), None), P("blk", None))
    return jax.shard_map(
        body, mesh=mesh, in_specs=in_specs, out_specs=P("blk", "wide"), check_vma=False
    )
```

```python
import functools
import math

import jax
import jax.numpy as jnp
import numpy as np
from jax import lax
from jax.experimental import pallas as pl
from jax.experimental.pallas import tpu as pltpu
from jax.sharding import PartitionSpec as P

MESH = pl.DeviceIdType.MESH
LANES = 128
SCREEN = 0.3
F32 = jnp.float32
BF16 = jnp.bfloat16


def basis(grid):
    half = grid // 2
    index = np.arange(grid)
    angle = 2.0 * math.pi / grid * ((index[:, None] * index[None, :]) % grid)
    cosines = np.cos(angle).astype(np.float32).astype(BF16).astype(np.float32)
    sines = np.sin(angle).astype(np.float32).astype(BF16).astype(np.float32)
    odd = np.arange(1, (grid + 1) // 2)
    q = np.concatenate([cosines[: half + 1], sines[odd]], axis=0)
    freq = np.concatenate([index[: half + 1], odd])
    weight = np.where(np.isin(freq, odd), 2.0, 1.0)
    return q, freq, weight


def plan(grid):
    q, freq, weight = basis(grid)
    group = max(d for d in range(1, grid + 1) if grid % d == 0 and d * grid <= 2 * LANES)
    per = grid // group
    wide = 2 * LANES
    a_mat = np.kron(q, np.eye(per))
    b_mat = np.kron(np.eye(group), q)
    c_mat = np.zeros((2, wide, group, LANES), np.float32)
    for h in range(2):
        lane = h * (LANES // 2)
        for j in range(group):
            c_mat[h, j * grid : (j + 1) * grid, j, lane : lane + grid] = q.T
    c_mat = c_mat.reshape(2 * wide, group * LANES)
    wave = 2.0 * math.pi / grid * freq
    sq = wave * wave
    total = sq[:, None, None] + sq[None, :, None] + sq[None, None, :]
    kern = 4.0 * math.pi / (total + SCREEN * SCREEN) / float(grid**3)
    kern = kern * weight[:, None, None] * weight[None, :, None] * weight[None, None, :]
    packed = np.zeros((grid // 2, grid, 2, LANES // 2), np.float32)
    for h in range(2):
        packed[:, :, h, :grid] = kern[h * (grid // 2) : (h + 1) * (grid // 2)]
    packed = packed.reshape(grid // 2 * grid, LANES)
    mats = [a_mat, a_mat.T, b_mat, b_mat.T, c_mat, c_mat.T]
    return group, [m.astype(BF16) for m in mats] + [packed.astype(np.float32)]


def dot(x, y):
    return jnp.dot(x, y, preferred_element_type=F32)


def exchange(pair, tables, y_ref, grid, group):
    a_ref, at_ref, b_ref, bt_ref, c_ref, ct_ref, k_ref = tables
    rows, wide = pair.shape
    hrows = rows // 2
    z = dot(a_ref[...], pair).astype(BF16)
    z = jnp.concatenate([z[:hrows], z[hrows:]], axis=1)
    y = dot(z, c_ref[...])
    for j in range(group):
        y_ref[pl.ds(j, hrows, stride=group), :] = y[:, j * LANES : (j + 1) * LANES]
    block = group * grid
    chunks = y_ref.shape[0] // block
    for i in range(0, chunks, 2):
        spans = [pl.ds(k * block, block) for k in (i, i + 1)]
        x = jnp.concatenate([y_ref[s, :].astype(BF16) for s in spans], axis=1)
        kern = jnp.concatenate([k_ref[s, :] for s in spans], axis=1)
        spec = (dot(b_ref[...], x) * kern).astype(BF16)
        back = dot(bt_ref[...], spec)
        for n, s in enumerate(spans):
            y_ref[s, :] = back[:, n * LANES : (n + 1) * LANES]
    x = jnp.concatenate(
        [y_ref[pl.ds(j, hrows, stride=group), :].astype(BF16) for j in range(group)], axis=1
    )
    z = dot(x, ct_ref[...]).astype(BF16)
    z = jnp.concatenate([z[:, :wide], z[:, wide:]], axis=0)
    return dot(at_ref[...], z)


def relaid(raw_ref, flat_ref, z_ref, width):
    for first in range(0, flat_ref.shape[0], 8):
        some = min(8, flat_ref.shape[0] - first)
        part = raw_ref[:, first * LANES : (first + some) * LANES]
        flat_ref[first : first + some, :] = part.astype(F32).reshape(some, LANES)
    period = math.lcm(width, LANES)
    tiles = period // LANES
    lines = period // width
    count = flat_ref.shape[0] // tiles
    columns = [flat_ref[pl.ds(t, count, stride=tiles), :] for t in range(tiles)]
    lane = lax.broadcasted_iota(jnp.int32, (count, LANES), 1)
    for j in range(lines):
        first, shift = divmod(width * j, LANES)
        need = max(2, -(-(shift + width) // LANES))
        x = jnp.concatenate(columns[first : first + need], axis=1)
        if shift:
            x = pltpu.roll(x, need * LANES - shift, 1)
        for half in range(2):
            piece = x[:, half * LANES : (half + 1) * LANES]
            piece = jnp.where(lane + half * LANES < width, piece, 0.0)
            z_ref[half, pl.ds(j, count, stride=lines), :] = piece
    return jnp.concatenate([z_ref[0], z_ref[1]], axis=1)


def partners(w, n_wide):
    if n_wide & (n_wide - 1):
        return [(lax.rem(w + d, n_wide), d - 1) for d in range(1, n_wide)]
    bits = [1 << k for k in range(n_wide.bit_length() - 1)]
    found = []
    for d in range(1, n_wide):
        flips = [bit for bit in bits if d & bit]
        other = w
        for bit in flips:
            other = other + bit - 2 * bit * lax.rem(w // bit, 2)
        found.append((len([bit for bit in flips if bit > 1]), d, other))
    found.sort(key=lambda item: (-item[0], item[1]))
    return [(other, d - 1) for _, d, other in found]


def kernel(n_wide, n_blk, grid, group, src_hbm, tgt_hbm, *rest):
    table_hbm = rest[:7]
    out_ref = rest[7]
    tables = rest[8:15]
    (src_ref, tgt_ref, y_ref, flat_ref, z_ref, source_ref, tgt_out, tgt_in, total, parts_out, parts_in,
     passed_out, passed_in, raw_sem, table_sem, send_sem, recv_sem) = rest[15:]
    w = lax.axis_index("wide")
    b = lax.axis_index("blk")
    width = group * grid
    raw = [
        pltpu.make_async_copy(hbm, ref, raw_sem.at[i])
        for i, (hbm, ref) in enumerate(((tgt_hbm, tgt_ref), (src_hbm, src_ref)))
    ]
    for load in raw:
        load.start()
    loads = [
        pltpu.make_async_copy(hbm, ref, table_sem.at[i])
        for i, (hbm, ref) in enumerate(zip(table_hbm, tables))
    ]
    core = lax.rem(w, 2)
    ahead = (w, lax.rem(b + 1, n_blk))
    behind = (w, lax.rem(b + n_blk - 1, n_blk))
    partner = (w + 1 - 2 * core, b)
    peers = partners(w, n_wide)
    barrier = pltpu.get_barrier_semaphore()
    greeted = [ahead, behind] + [(other, b) for other, _ in peers]
    for device in greeted:
        pl.semaphore_signal(barrier, inc=1, device_id=device, device_id_type=MESH)

    def send(src, dst, slot, device):
        copy = pltpu.make_async_remote_copy(
            src_ref=src, dst_ref=dst, send_sem=send_sem.at[slot], recv_sem=recv_sem.at[slot],
            device_id=device, device_id_type=MESH,
        )
        copy.start()
        return copy

    for load in loads:
        load.start()
    raw[0].wait()
    target = relaid(tgt_ref, flat_ref, z_ref, width)
    tgt_out[...] = target.reshape(tgt_out.shape).astype(BF16)
    quarter = tgt_out.shape[0] // 2
    pl.semaphore_wait(barrier, len(greeted))
    hops = [
        send(tgt_out.at[core * quarter + k], tgt_in.at[core * quarter + k], k, ahead)
        for k in range(quarter)
    ]
    raw[1].wait()
    source = relaid(src_ref, flat_ref, z_ref, width)
    source_ref[...] = source
    for load in loads:
        load.wait()
    rows = source.shape[0] // n_wide

    def scatter(target, turn):
        pair = (source_ref[...] * target).astype(BF16)
        term = source_ref[...] * exchange(pair, tables, y_ref, grid, group)
        for k in range(n_wide):
            piece = term[k * rows : (k + 1) * rows]
            total[turn, k] = piece
            parts_out[turn, k] = piece.astype(BF16)
        slot = 2 * quarter + 1 + turn * (n_wide - 1)
        return [
            send(parts_out.at[turn, other], parts_in.at[turn, d], slot + d, (other, b))
            for other, d in peers
        ]

    def gathered(copies, turn):
        summed = total[turn, w]
        for (_, d), copy in reversed(list(zip(peers, copies))):
            copy.wait()
            summed = summed + parts_in[turn, d].astype(F32)
        return summed

    first = scatter(target, 0)
    relays = []
    for k, hop in enumerate(hops):
        hop.wait()
        here = tgt_in.at[core * quarter + k]
        relays.append(send(here, here, quarter + k, partner))
    for relay in relays:
        relay.wait()
    second = scatter(tgt_in[...].astype(F32).reshape(source.shape), 1)
    passed_out[...] = gathered(first, 0).astype(BF16)
    passed = send(passed_out, passed_in, 2 * quarter, ahead)
    summed = gathered(second, 1)
    passed.wait()
    summed = summed + passed_in[...].astype(F32)
    for k in range(rows):
        out_ref[0:1, k * width : (k + 1) * width] = summed[k : k + 1, :width]


def shards(n_wide, n_blk, sources, targets):
    cells = sources.shape[1]
    grid = round(cells ** (1.0 / 3.0))
    group, tables = plan(grid)
    wide = 2 * LANES
    rows = cells // (group * grid)
    part = rows // n_wide
    line = 8 * (rows // 64)
    vmem = pl.BlockSpec(memory_space=pltpu.VMEM)
    hbm = pl.BlockSpec(memory_space=pltpu.HBM)
    sems = 2 * (rows // line // 2) + 1 + 2 * (n_wide - 1)
    result = pl.pallas_call(
        functools.partial(kernel, n_wide, n_blk, grid, group),
        out_shape=pltpu.VMEM((1, cells // n_wide), F32),
        in_specs=[hbm] * 9,
        out_specs=vmem,
        scratch_shapes=[pltpu.VMEM(t.shape, t.dtype) for t in tables]
        + [
            pltpu.VMEM((1, cells), BF16),
            pltpu.VMEM((1, cells), BF16),
            pltpu.VMEM((rows // 2 * group, LANES), F32),
            pltpu.VMEM((cells // LANES, LANES), F32),
            pltpu.VMEM((2, rows, LANES), F32),
            pltpu.VMEM((rows, wide), F32),
            pltpu.VMEM((rows // line, line, wide), BF16),
            pltpu.VMEM((rows // line, line, wide), BF16),
            pltpu.VMEM((2, n_wide, part, wide), F32),
            pltpu.VMEM((2, n_wide, part, wide), BF16),
            pltpu.VMEM((2, n_wide - 1, part, wide), BF16),
            pltpu.VMEM((part, wide), BF16),
            pltpu.VMEM((part, wide), BF16),
            pltpu.SemaphoreType.DMA((2,)),
            pltpu.SemaphoreType.DMA((len(tables),)),
            pltpu.SemaphoreType.DMA((sems,)),
            pltpu.SemaphoreType.DMA((sems,)),
        ],
        compiler_params=pltpu.CompilerParams(collective_id=0, has_side_effects=True, vmem_limit_bytes=56 << 20),
    )(sources, targets, *[jnp.asarray(t) for t in tables])
    return -result


def solution(mesh):
    body = functools.partial(shards, mesh.shape["wide"], mesh.shape["blk"])
    in_specs = (P(("wide", "blk"), None), P("blk", None))
    return jax.shard_map(
        body, mesh=mesh, in_specs=in_specs, out_specs=P("blk", "wide"), check_vma=False
    )
```

```python
import functools
import math

import jax
import jax.numpy as jnp
import numpy as np
from jax import lax
from jax.experimental import pallas as pl
from jax.experimental.pallas import tpu as pltpu
from jax.sharding import PartitionSpec as P

MESH = pl.DeviceIdType.MESH
LANES = 128
SCREEN = 0.3
F32 = jnp.float32
BF16 = jnp.bfloat16


def basis(grid):
    half = grid // 2
    index = np.arange(grid)
    angle = 2.0 * math.pi / grid * ((index[:, None] * index[None, :]) % grid)
    cosines = np.cos(angle).astype(np.float32).astype(BF16).astype(np.float32)
    sines = np.sin(angle).astype(np.float32).astype(BF16).astype(np.float32)
    odd = np.arange(1, (grid + 1) // 2)
    q = np.concatenate([cosines[: half + 1], sines[odd]], axis=0)
    freq = np.concatenate([index[: half + 1], odd])
    weight = np.where(np.isin(freq, odd), 2.0, 1.0)
    return q, freq, weight


def plan(grid):
    q, freq, weight = basis(grid)
    group = max(d for d in range(1, grid + 1) if grid % d == 0 and d * grid <= 2 * LANES)
    per = grid // group
    wide = 2 * LANES
    a_mat = np.kron(q, np.eye(per))
    b_mat = np.kron(np.eye(group), q)
    c_mat = np.zeros((2, wide, group, LANES), np.float32)
    for h in range(2):
        lane = h * (LANES // 2)
        for j in range(group):
            c_mat[h, j * grid : (j + 1) * grid, j, lane : lane + grid] = q.T
    c_mat = c_mat.reshape(2 * wide, group * LANES)
    wave = 2.0 * math.pi / grid * freq
    sq = wave * wave
    total = sq[:, None, None] + sq[None, :, None] + sq[None, None, :]
    kern = 4.0 * math.pi / (total + SCREEN * SCREEN) / float(grid**3)
    kern = kern * weight[:, None, None] * weight[None, :, None] * weight[None, None, :]
    packed = np.zeros((grid // 2, grid, 2, LANES // 2), np.float32)
    for h in range(2):
        packed[:, :, h, :grid] = kern[h * (grid // 2) : (h + 1) * (grid // 2)]
    packed = packed.reshape(grid // 2 * grid, LANES)
    mats = [a_mat, a_mat.T, b_mat, b_mat.T, c_mat, c_mat.T]
    return group, [m.astype(BF16) for m in mats] + [packed.astype(np.float32)]


def dot(x, y):
    return jnp.dot(x, y, preferred_element_type=F32)


def exchange(pair, tables, y_ref, grid, group):
    a_ref, at_ref, b_ref, bt_ref, c_ref, ct_ref, k_ref = tables
    rows, wide = pair.shape
    hrows = rows // 2
    z = dot(a_ref[...], pair).astype(BF16)
    z = jnp.concatenate([z[:hrows], z[hrows:]], axis=1)
    y = dot(z, c_ref[...])
    for j in range(group):
        y_ref[pl.ds(j, hrows, stride=group), :] = y[:, j * LANES : (j + 1) * LANES]
    block = group * grid
    chunks = y_ref.shape[0] // block
    for i in range(0, chunks, 2):
        spans = [pl.ds(k * block, block) for k in (i, i + 1)]
        x = jnp.concatenate([y_ref[s, :].astype(BF16) for s in spans], axis=1)
        kern = jnp.concatenate([k_ref[s, :] for s in spans], axis=1)
        spec = (dot(b_ref[...], x) * kern).astype(BF16)
        back = dot(bt_ref[...], spec)
        for n, s in enumerate(spans):
            y_ref[s, :] = back[:, n * LANES : (n + 1) * LANES]
    x = jnp.concatenate(
        [y_ref[pl.ds(j, hrows, stride=group), :].astype(BF16) for j in range(group)], axis=1
    )
    z = dot(x, ct_ref[...]).astype(BF16)
    z = jnp.concatenate([z[:, :wide], z[:, wide:]], axis=0)
    return dot(at_ref[...], z)


def flattened(raw_ref, flat_ref):
    lines = raw_ref.shape[1] // LANES
    for first in range(0, lines, 8):
        some = min(8, lines - first)
        part = raw_ref[:, first * LANES : (first + some) * LANES]
        flat_ref[first : first + some, :] = part.astype(F32).reshape(some, LANES)
    if flat_ref.shape[0] > lines:
        flat_ref[lines:, :] = jnp.zeros((flat_ref.shape[0] - lines, LANES), F32)


def relaid(flat_ref, z_ref, width):
    period = math.lcm(width, LANES)
    tiles = period // LANES
    lines = period // width
    count = z_ref.shape[1] // lines
    columns = [flat_ref[pl.ds(t, count, stride=tiles), :] for t in range(tiles)]
    lane = lax.broadcasted_iota(jnp.int32, (count, LANES), 1)
    for j in range(lines):
        first, shift = divmod(width * j, LANES)
        need = max(2, -(-(shift + width) // LANES))
        x = jnp.concatenate(columns[first : first + need], axis=1)
        if shift:
            x = pltpu.roll(x, need * LANES - shift, 1)
        for half in range(2):
            piece = x[:, half * LANES : (half + 1) * LANES]
            piece = jnp.where(lane + half * LANES < width, piece, 0.0)
            z_ref[half, pl.ds(j, count, stride=lines), :] = piece
    return jnp.concatenate([z_ref[0], z_ref[1]], axis=1)


def partners(w, n_wide):
    if n_wide & (n_wide - 1):
        return [(lax.rem(w + d, n_wide), d - 1) for d in range(1, n_wide)]
    bits = [1 << k for k in range(n_wide.bit_length() - 1)]
    found = []
    for d in range(1, n_wide):
        flips = [bit for bit in bits if d & bit]
        other = w
        for bit in flips:
            other = other + bit - 2 * bit * lax.rem(w // bit, 2)
        found.append((len([bit for bit in flips if bit > 1]), d, other))
    found.sort(key=lambda item: (-item[0], item[1]))
    return [(other, d - 1) for _, d, other in found]


def kernel(n_wide, n_blk, grid, group, src_hbm, tgt_hbm, *rest):
    table_hbm = rest[:7]
    out_ref = rest[7]
    tables = rest[8:15]
    (src_ref, tgt_ref, y_ref, flat_ref, z_ref, source_ref, tgt_out, tgt_in, total, parts_out, parts_in,
     passed_out, passed_in, raw_sem, table_sem, send_sem, recv_sem) = rest[15:]
    w = lax.axis_index("wide")
    b = lax.axis_index("blk")
    width = group * grid
    raw = [
        pltpu.make_async_copy(hbm, ref, raw_sem.at[i])
        for i, (hbm, ref) in enumerate(((tgt_hbm, tgt_ref), (src_hbm, src_ref)))
    ]
    for load in raw:
        load.start()
    loads = [
        pltpu.make_async_copy(hbm, ref, table_sem.at[i])
        for i, (hbm, ref) in enumerate(zip(table_hbm, tables))
    ]
    core = lax.rem(w, 2)
    ahead = (w, lax.rem(b + 1, n_blk))
    behind = (w, lax.rem(b + n_blk - 1, n_blk))
    partner = (w + 1 - 2 * core, b)
    across = (partner[0], ahead[1])
    peers = partners(w, n_wide)
    barrier = pltpu.get_barrier_semaphore()
    greeted = [ahead, behind, across, (partner[0], behind[1])] + [(other, b) for other, _ in peers]
    for device in greeted:
        pl.semaphore_signal(barrier, inc=1, device_id=device, device_id_type=MESH)

    def send(src, dst, slot, device):
        copy = pltpu.make_async_remote_copy(
            src_ref=src, dst_ref=dst, send_sem=send_sem.at[slot], recv_sem=recv_sem.at[slot],
            device_id=device, device_id_type=MESH,
        )
        copy.start()
        return copy

    for load in loads:
        load.start()
    raw[0].wait()
    flattened(tgt_ref, flat_ref)
    tgt_out[...] = flat_ref[...].astype(BF16).reshape(tgt_out.shape)
    quarter = tgt_out.shape[0] // 2
    mine = core * quarter
    last = mine + quarter - 1
    pl.semaphore_wait(barrier, len(greeted))
    hops = [send(tgt_out.at[mine + k], tgt_in.at[mine + k], k, ahead) for k in range(quarter)]
    direct = send(tgt_out.at[last], tgt_in.at[last], 2 * quarter - 1, across)
    target = relaid(flat_ref, z_ref, width)
    raw[1].wait()
    flattened(src_ref, flat_ref)
    source = relaid(flat_ref, z_ref, width)
    source_ref[...] = source
    for load in loads:
        load.wait()
    rows = source.shape[0] // n_wide

    def scatter(target, turn):
        pair = (source_ref[...] * target).astype(BF16)
        term = source_ref[...] * exchange(pair, tables, y_ref, grid, group)
        for k in range(n_wide):
            piece = term[k * rows : (k + 1) * rows]
            total[turn, k] = piece
            parts_out[turn, k] = piece.astype(BF16)
        slot = 2 * quarter + 1 + turn * (n_wide - 1)
        return [
            send(parts_out.at[turn, other], parts_in.at[turn, d], slot + d, (other, b))
            for other, d in peers
        ]

    def gathered(copies, turn):
        summed = total[turn, w]
        for (_, d), copy in reversed(list(zip(peers, copies))):
            copy.wait()
            summed = summed + parts_in[turn, d].astype(F32)
        return summed

    first = scatter(target, 0)
    relays = []
    for k, hop in enumerate(hops):
        hop.wait()
        if k < quarter - 1:
            here = tgt_in.at[mine + k]
            relays.append(send(here, here, quarter + k, partner))
    for relay in relays:
        relay.wait()
    direct.wait()
    flat_ref[...] = tgt_in[...].astype(F32).reshape(flat_ref.shape)
    second = scatter(relaid(flat_ref, z_ref, width), 1)
    passed_out[...] = gathered(first, 0).astype(BF16)
    passed = send(passed_out, passed_in, 2 * quarter, ahead)
    summed = gathered(second, 1)
    passed.wait()
    summed = summed + passed_in[...].astype(F32)
    for k in range(rows):
        out_ref[0:1, k * width : (k + 1) * width] = summed[k : k + 1, :width]


def shards(n_wide, n_blk, sources, targets):
    cells = sources.shape[1]
    grid = round(cells ** (1.0 / 3.0))
    group, tables = plan(grid)
    wide = 2 * LANES
    rows = cells // (group * grid)
    part = rows // n_wide
    line = 8 * -(-cells // (64 * LANES))
    vmem = pl.BlockSpec(memory_space=pltpu.VMEM)
    hbm = pl.BlockSpec(memory_space=pltpu.HBM)
    sems = 8 + 1 + 2 * (n_wide - 1)
    result = pl.pallas_call(
        functools.partial(kernel, n_wide, n_blk, grid, group),
        out_shape=pltpu.VMEM((1, cells // n_wide), F32),
        in_specs=[hbm] * 9,
        out_specs=vmem,
        scratch_shapes=[pltpu.VMEM(t.shape, t.dtype) for t in tables]
        + [
            pltpu.VMEM((1, cells), BF16),
            pltpu.VMEM((1, cells), BF16),
            pltpu.VMEM((rows // 2 * group, LANES), F32),
            pltpu.VMEM((8 * line, LANES), F32),
            pltpu.VMEM((2, rows, LANES), F32),
            pltpu.VMEM((rows, wide), F32),
            pltpu.VMEM((8, line, LANES), BF16),
            pltpu.VMEM((8, line, LANES), BF16),
            pltpu.VMEM((2, n_wide, part, wide), F32),
            pltpu.VMEM((2, n_wide, part, wide), BF16),
            pltpu.VMEM((2, n_wide - 1, part, wide), BF16),
            pltpu.VMEM((part, wide), BF16),
            pltpu.VMEM((part, wide), BF16),
            pltpu.SemaphoreType.DMA((2,)),
            pltpu.SemaphoreType.DMA((len(tables),)),
            pltpu.SemaphoreType.DMA((sems,)),
            pltpu.SemaphoreType.DMA((sems,)),
        ],
        compiler_params=pltpu.CompilerParams(collective_id=0, has_side_effects=True, vmem_limit_bytes=56 << 20),
    )(sources, targets, *[jnp.asarray(t) for t in tables])
    return -result


def solution(mesh):
    body = functools.partial(shards, mesh.shape["wide"], mesh.shape["blk"])
    in_specs = (P(("wide", "blk"), None), P("blk", None))
    return jax.shard_map(
        body, mesh=mesh, in_specs=in_specs, out_specs=P("blk", "wide"), check_vma=False
    )
```

```python
import functools
import math

import jax
import jax.numpy as jnp
import numpy as np
from jax import lax
from jax.experimental import pallas as pl
from jax.experimental.pallas import tpu as pltpu
from jax.sharding import PartitionSpec as P

MESH = pl.DeviceIdType.MESH
LANES = 128
SCREEN = 0.3
F32 = jnp.float32
BF16 = jnp.bfloat16


def basis(grid):
    half = grid // 2
    index = np.arange(grid)
    angle = 2.0 * math.pi / grid * ((index[:, None] * index[None, :]) % grid)
    cosines = np.cos(angle).astype(np.float32).astype(BF16).astype(np.float32)
    sines = np.sin(angle).astype(np.float32).astype(BF16).astype(np.float32)
    odd = np.arange(1, (grid + 1) // 2)
    q = np.concatenate([cosines[: half + 1], sines[odd]], axis=0)
    freq = np.concatenate([index[: half + 1], odd])
    weight = np.where(np.isin(freq, odd), 2.0, 1.0)
    return q, freq, weight


def plan(grid):
    q, freq, weight = basis(grid)
    group = max(d for d in range(1, grid + 1) if grid % d == 0 and d * grid <= 2 * LANES)
    per = grid // group
    wide = 2 * LANES
    a_mat = np.kron(q, np.eye(per))
    b_mat = np.kron(np.eye(group), q)
    c_mat = np.zeros((2, wide, group, LANES), np.float32)
    for h in range(2):
        lane = h * (LANES // 2)
        for j in range(group):
            c_mat[h, j * grid : (j + 1) * grid, j, lane : lane + grid] = q.T
    c_mat = c_mat.reshape(2 * wide, group * LANES)
    wave = 2.0 * math.pi / grid * freq
    sq = wave * wave
    total = sq[:, None, None] + sq[None, :, None] + sq[None, None, :]
    kern = 4.0 * math.pi / (total + SCREEN * SCREEN) / float(grid**3)
    kern = kern * weight[:, None, None] * weight[None, :, None] * weight[None, None, :]
    packed = np.zeros((grid // 2, grid, 2, LANES // 2), np.float32)
    for h in range(2):
        packed[:, :, h, :grid] = kern[h * (grid // 2) : (h + 1) * (grid // 2)]
    packed = packed.reshape(grid // 2 * grid, LANES)
    mats = [a_mat, a_mat.T, b_mat, b_mat.T, c_mat, c_mat.T]
    return group, [m.astype(BF16) for m in mats] + [packed.astype(np.float32)]


def dot(x, y):
    return jnp.dot(x, y, preferred_element_type=F32)


def exchange(pair, tables, y_ref, grid, group):
    a_ref, at_ref, b_ref, bt_ref, c_ref, ct_ref, k_ref = tables
    rows, wide = pair.shape
    hrows = rows // 2
    z = dot(a_ref[...], pair).astype(BF16)
    z = jnp.concatenate([z[:hrows], z[hrows:]], axis=1)
    y = dot(z, c_ref[...])
    for j in range(group):
        y_ref[pl.ds(j, hrows, stride=group), :] = y[:, j * LANES : (j + 1) * LANES]
    block = group * grid
    chunks = y_ref.shape[0] // block
    for i in range(0, chunks, 2):
        spans = [pl.ds(k * block, block) for k in (i, i + 1)]
        x = jnp.concatenate([y_ref[s, :].astype(BF16) for s in spans], axis=1)
        kern = jnp.concatenate([k_ref[s, :] for s in spans], axis=1)
        spec = (dot(b_ref[...], x) * kern).astype(BF16)
        back = dot(bt_ref[...], spec)
        for n, s in enumerate(spans):
            y_ref[s, :] = back[:, n * LANES : (n + 1) * LANES]
    x = jnp.concatenate(
        [y_ref[pl.ds(j, hrows, stride=group), :].astype(BF16) for j in range(group)], axis=1
    )
    z = dot(x, ct_ref[...]).astype(BF16)
    z = jnp.concatenate([z[:, :wide], z[:, wide:]], axis=0)
    return dot(at_ref[...], z)


def flattened(raw_ref, flat_ref):
    lines = raw_ref.shape[1] // LANES
    for first in range(0, lines, 8):
        some = min(8, lines - first)
        part = raw_ref[:, first * LANES : (first + some) * LANES]
        flat_ref[first : first + some, :] = part.astype(F32).reshape(some, LANES)
    if flat_ref.shape[0] > lines:
        flat_ref[lines:, :] = jnp.zeros((flat_ref.shape[0] - lines, LANES), F32)


def relaid(flat_ref, z_ref, width):
    period = math.lcm(width, LANES)
    tiles = period // LANES
    lines = period // width
    count = z_ref.shape[1] // lines
    columns = [flat_ref[pl.ds(t, count, stride=tiles), :] for t in range(tiles)]
    lane = lax.broadcasted_iota(jnp.int32, (count, LANES), 1)
    for j in range(lines):
        first, shift = divmod(width * j, LANES)
        need = max(2, -(-(shift + width) // LANES))
        x = jnp.concatenate(columns[first : first + need], axis=1)
        if shift:
            x = pltpu.roll(x, need * LANES - shift, 1)
        for half in range(2):
            piece = x[:, half * LANES : (half + 1) * LANES]
            piece = jnp.where(lane + half * LANES < width, piece, 0.0)
            z_ref[half, pl.ds(j, count, stride=lines), :] = piece
    return jnp.concatenate([z_ref[0], z_ref[1]], axis=1)


def partners(w, n_wide):
    if n_wide & (n_wide - 1):
        return [(lax.rem(w + d, n_wide), d - 1) for d in range(1, n_wide)]
    bits = [1 << k for k in range(n_wide.bit_length() - 1)]
    found = []
    for d in range(1, n_wide):
        flips = [bit for bit in bits if d & bit]
        other = w
        for bit in flips:
            other = other + bit - 2 * bit * lax.rem(w // bit, 2)
        found.append((len([bit for bit in flips if bit > 1]), d, other))
    found.sort(key=lambda item: (-item[0], item[1]))
    return [(other, d - 1) for _, d, other in found]


def kernel(n_wide, n_blk, grid, group, src_hbm, tgt_hbm, *rest):
    table_hbm = rest[:7]
    out_ref = rest[7]
    tables = rest[8:15]
    (src_ref, tgt_ref, y_ref, flat_ref, z_ref, source_ref, tgt_out, tgt_in, total, parts_out, parts_in,
     passed_out, passed_in, raw_sem, table_sem, send_sem, recv_sem) = rest[15:]
    w = lax.axis_index("wide")
    b = lax.axis_index("blk")
    width = group * grid
    raw = [
        pltpu.make_async_copy(hbm, ref, raw_sem.at[i])
        for i, (hbm, ref) in enumerate(((tgt_hbm, tgt_ref), (src_hbm, src_ref)))
    ]
    for load in raw:
        load.start()
    loads = [
        pltpu.make_async_copy(hbm, ref, table_sem.at[i])
        for i, (hbm, ref) in enumerate(zip(table_hbm, tables))
    ]
    core = lax.rem(w, 2)
    ahead = (w, lax.rem(b + 1, n_blk))
    behind = (w, lax.rem(b + n_blk - 1, n_blk))
    partner = (w + 1 - 2 * core, b)
    across = (partner[0], ahead[1])
    peers = partners(w, n_wide)
    barrier = pltpu.get_barrier_semaphore()
    greeted = [behind, (partner[0], behind[1])] + [(other, b) for other, _ in peers]
    for device in greeted:
        pl.semaphore_signal(barrier, inc=1, device_id=device, device_id_type=MESH)

    def send(src, dst, slot, device):
        copy = pltpu.make_async_remote_copy(
            src_ref=src, dst_ref=dst, send_sem=send_sem.at[slot], recv_sem=recv_sem.at[slot],
            device_id=device, device_id_type=MESH,
        )
        copy.start()
        return copy

    for load in loads:
        load.start()
    raw[0].wait()
    flattened(tgt_ref, flat_ref)
    tgt_out[...] = flat_ref[...].astype(BF16).reshape(tgt_out.shape)
    quarter = tgt_out.shape[0] // 2
    mine = core * quarter
    last = mine + quarter - 1
    pl.semaphore_wait(barrier, len(greeted))
    hops = [send(tgt_out.at[mine + k], tgt_in.at[mine + k], k, ahead) for k in range(quarter)]
    direct = send(tgt_out.at[last], tgt_in.at[last], 2 * quarter - 1, across)
    target = relaid(flat_ref, z_ref, width)
    raw[1].wait()
    flattened(src_ref, flat_ref)
    source = relaid(flat_ref, z_ref, width)
    source_ref[...] = source
    for load in loads:
        load.wait()
    rows = source.shape[0] // n_wide

    def scatter(target, turn):
        pair = (source_ref[...] * target).astype(BF16)
        term = source_ref[...] * exchange(pair, tables, y_ref, grid, group)
        for k in range(n_wide):
            piece = term[k * rows : (k + 1) * rows]
            total[turn, k] = piece
            parts_out[turn, k] = piece.astype(BF16)
        slot = 2 * quarter + 1 + turn * (n_wide - 1)
        return [
            send(parts_out.at[turn, other], parts_in.at[turn, d], slot + d, (other, b))
            for other, d in peers
        ]

    def gathered(copies, turn):
        summed = total[turn, w]
        for (_, d), copy in reversed(list(zip(peers, copies))):
            copy.wait()
            summed = summed + parts_in[turn, d].astype(F32)
        return summed

    first = scatter(target, 0)
    relays = []
    for k, hop in enumerate(hops):
        hop.wait()
        if k < quarter - 1:
            here = tgt_in.at[mine + k]
            relays.append(send(here, here, quarter + k, partner))
    for relay in relays:
        relay.wait()
    direct.wait()
    flat_ref[...] = tgt_in[...].astype(F32).reshape(flat_ref.shape)
    second = scatter(relaid(flat_ref, z_ref, width), 1)
    passed_out[...] = gathered(first, 0).astype(BF16)
    passed = send(passed_out, passed_in, 2 * quarter, ahead)
    summed = gathered(second, 1)
    passed.wait()
    summed = summed + passed_in[...].astype(F32)
    for k in range(rows):
        out_ref[0:1, k * width : (k + 1) * width] = summed[k : k + 1, :width]


def shards(n_wide, n_blk, sources, targets):
    cells = sources.shape[1]
    grid = round(cells ** (1.0 / 3.0))
    group, tables = plan(grid)
    wide = 2 * LANES
    rows = cells // (group * grid)
    part = rows // n_wide
    line = 8 * -(-cells // (64 * LANES))
    vmem = pl.BlockSpec(memory_space=pltpu.VMEM)
    hbm = pl.BlockSpec(memory_space=pltpu.HBM)
    sems = 8 + 1 + 2 * (n_wide - 1)
    result = pl.pallas_call(
        functools.partial(kernel, n_wide, n_blk, grid, group),
        out_shape=pltpu.VMEM((1, cells // n_wide), F32),
        in_specs=[hbm] * 9,
        out_specs=vmem,
        scratch_shapes=[pltpu.VMEM(t.shape, t.dtype) for t in tables]
        + [
            pltpu.VMEM((1, cells), BF16),
            pltpu.VMEM((1, cells), BF16),
            pltpu.VMEM((rows // 2 * group, LANES), F32),
            pltpu.VMEM((8 * line, LANES), F32),
            pltpu.VMEM((2, rows, LANES), F32),
            pltpu.VMEM((rows, wide), F32),
            pltpu.VMEM((8, line, LANES), BF16),
            pltpu.VMEM((8, line, LANES), BF16),
            pltpu.VMEM((2, n_wide, part, wide), F32),
            pltpu.VMEM((2, n_wide, part, wide), BF16),
            pltpu.VMEM((2, n_wide - 1, part, wide), BF16),
            pltpu.VMEM((part, wide), BF16),
            pltpu.VMEM((part, wide), BF16),
            pltpu.SemaphoreType.DMA((2,)),
            pltpu.SemaphoreType.DMA((len(tables),)),
            pltpu.SemaphoreType.DMA((sems,)),
            pltpu.SemaphoreType.DMA((sems,)),
        ],
        compiler_params=pltpu.CompilerParams(collective_id=0, has_side_effects=True, vmem_limit_bytes=56 << 20),
    )(sources, targets, *[jnp.asarray(t) for t in tables])
    return -result


def solution(mesh):
    body = functools.partial(shards, mesh.shape["wide"], mesh.shape["blk"])
    in_specs = (P(("wide", "blk"), None), P("blk", None))
    return jax.shard_map(
        body, mesh=mesh, in_specs=in_specs, out_specs=P("blk", "wide"), check_vma=False
    )
```

```python
import functools
import math

import jax
import jax.numpy as jnp
import numpy as np
from jax import lax
from jax.experimental import pallas as pl
from jax.experimental.pallas import tpu as pltpu
from jax.sharding import PartitionSpec as P

MESH = pl.DeviceIdType.MESH
LANES = 128
SCREEN = 0.3
F32 = jnp.float32
BF16 = jnp.bfloat16


def basis(grid):
    half = grid // 2
    index = np.arange(grid)
    angle = 2.0 * math.pi / grid * ((index[:, None] * index[None, :]) % grid)
    cosines = np.cos(angle).astype(np.float32).astype(BF16).astype(np.float32)
    sines = np.sin(angle).astype(np.float32).astype(BF16).astype(np.float32)
    odd = np.arange(1, (grid + 1) // 2)
    q = np.concatenate([cosines[: half + 1], sines[odd]], axis=0)
    freq = np.concatenate([index[: half + 1], odd])
    weight = np.where(np.isin(freq, odd), 2.0, 1.0)
    return q, freq, weight


def plan(grid):
    q, freq, weight = basis(grid)
    group = max(d for d in range(1, grid + 1) if grid % d == 0 and d * grid <= 2 * LANES)
    per = grid // group
    wide = 2 * LANES
    a_mat = np.kron(q, np.eye(per))
    b_mat = np.kron(np.eye(group), q)
    c_mat = np.zeros((2, wide, group, LANES), np.float32)
    for h in range(2):
        lane = h * (LANES // 2)
        for j in range(group):
            c_mat[h, j * grid : (j + 1) * grid, j, lane : lane + grid] = q.T
    c_mat = c_mat.reshape(2 * wide, group * LANES)
    wave = 2.0 * math.pi / grid * freq
    sq = wave * wave
    total = sq[:, None, None] + sq[None, :, None] + sq[None, None, :]
    kern = 4.0 * math.pi / (total + SCREEN * SCREEN) / float(grid**3)
    kern = kern * weight[:, None, None] * weight[None, :, None] * weight[None, None, :]
    packed = np.zeros((grid // 2, grid, 2, LANES // 2), np.float32)
    for h in range(2):
        packed[:, :, h, :grid] = kern[h * (grid // 2) : (h + 1) * (grid // 2)]
    packed = packed.reshape(grid // 2 * grid, LANES)
    mats = [a_mat, a_mat.T, b_mat, b_mat.T, c_mat, c_mat.T]
    return group, [m.astype(BF16) for m in mats] + [packed.astype(np.float32)]


def dot(x, y):
    return jnp.dot(x, y, preferred_element_type=F32)


def exchange(pair, tables, y_ref, grid, group):
    a_ref, at_ref, b_ref, bt_ref, c_ref, ct_ref, k_ref = tables
    rows, wide = pair.shape
    hrows = rows // 2
    z = dot(a_ref[...], pair).astype(BF16)
    z = jnp.concatenate([z[:hrows], z[hrows:]], axis=1)
    y = dot(z, c_ref[...])
    for j in range(group):
        y_ref[pl.ds(j, hrows, stride=group), :] = y[:, j * LANES : (j + 1) * LANES]
    block = group * grid
    chunks = y_ref.shape[0] // block
    for i in range(0, chunks, 2):
        spans = [pl.ds(k * block, block) for k in (i, i + 1)]
        x = jnp.concatenate([y_ref[s, :].astype(BF16) for s in spans], axis=1)
        kern = jnp.concatenate([k_ref[s, :] for s in spans], axis=1)
        spec = (dot(b_ref[...], x) * kern).astype(BF16)
        back = dot(bt_ref[...], spec)
        for n, s in enumerate(spans):
            y_ref[s, :] = back[:, n * LANES : (n + 1) * LANES]
    x = jnp.concatenate(
        [y_ref[pl.ds(j, hrows, stride=group), :].astype(BF16) for j in range(group)], axis=1
    )
    z = dot(x, ct_ref[...]).astype(BF16)
    z = jnp.concatenate([z[:, :wide], z[:, wide:]], axis=0)
    return dot(at_ref[...], z)


def flattened(raw_ref, flat_ref):
    lines = raw_ref.shape[1] // LANES
    for first in range(0, lines, 8):
        some = min(8, lines - first)
        part = raw_ref[:, first * LANES : (first + some) * LANES]
        flat_ref[first : first + some, :] = part.astype(F32).reshape(some, LANES)
    if flat_ref.shape[0] > lines:
        flat_ref[lines:, :] = jnp.zeros((flat_ref.shape[0] - lines, LANES), F32)


def relaid(flat_ref, z_ref, width):
    period = math.lcm(width, LANES)
    tiles = period // LANES
    lines = period // width
    count = z_ref.shape[1] // lines
    columns = [flat_ref[pl.ds(t, count, stride=tiles), :] for t in range(tiles)]
    lane = lax.broadcasted_iota(jnp.int32, (count, LANES), 1)
    for j in range(lines):
        first, shift = divmod(width * j, LANES)
        need = max(2, -(-(shift + width) // LANES))
        x = jnp.concatenate(columns[first : first + need], axis=1)
        if shift:
            x = pltpu.roll(x, need * LANES - shift, 1)
        for half in range(2):
            piece = x[:, half * LANES : (half + 1) * LANES]
            piece = jnp.where(lane + half * LANES < width, piece, 0.0)
            z_ref[half, pl.ds(j, count, stride=lines), :] = piece
    return jnp.concatenate([z_ref[0], z_ref[1]], axis=1)


def partners(w, n_wide):
    if n_wide & (n_wide - 1):
        return [(lax.rem(w + d, n_wide), d - 1) for d in range(1, n_wide)]
    bits = [1 << k for k in range(n_wide.bit_length() - 1)]
    found = []
    for d in range(1, n_wide):
        flips = [bit for bit in bits if d & bit]
        other = w
        for bit in flips:
            other = other + bit - 2 * bit * lax.rem(w // bit, 2)
        found.append((len([bit for bit in flips if bit > 1]), d, other))
    found.sort(key=lambda item: (-item[0], item[1]))
    return [(other, d - 1) for _, d, other in found]


def kernel(n_wide, n_blk, grid, group, src_hbm, tgt_hbm, *rest):
    table_hbm = rest[:7]
    out_ref = rest[7]
    tables = rest[8:15]
    (src_ref, tgt_ref, y_ref, flat_ref, z_ref, source_ref, tgt_out, tgt_in, parts_out, parts_in,
     passed_out, passed_in, raw_sem, table_sem, send_sem, recv_sem) = rest[15:]
    w = lax.axis_index("wide")
    b = lax.axis_index("blk")
    width = group * grid
    raw = [
        pltpu.make_async_copy(hbm, ref, raw_sem.at[i])
        for i, (hbm, ref) in enumerate(((tgt_hbm, tgt_ref), (src_hbm, src_ref)))
    ]
    for load in raw:
        load.start()
    loads = [
        pltpu.make_async_copy(hbm, ref, table_sem.at[i])
        for i, (hbm, ref) in enumerate(zip(table_hbm, tables))
    ]
    core = lax.rem(w, 2)
    ahead = (w, lax.rem(b + 1, n_blk))
    behind = (w, lax.rem(b + n_blk - 1, n_blk))
    partner = (w + 1 - 2 * core, b)
    across = (partner[0], ahead[1])
    peers = partners(w, n_wide)
    barrier = pltpu.get_barrier_semaphore()
    greeted = [behind, (partner[0], behind[1])] + [(other, b) for other, _ in peers]
    for device in greeted:
        pl.semaphore_signal(barrier, inc=1, device_id=device, device_id_type=MESH)

    def send(src, dst, slot, device):
        copy = pltpu.make_async_remote_copy(
            src_ref=src, dst_ref=dst, send_sem=send_sem.at[slot], recv_sem=recv_sem.at[slot],
            device_id=device, device_id_type=MESH,
        )
        copy.start()
        return copy

    for load in loads:
        load.start()
    raw[0].wait()
    flattened(tgt_ref, flat_ref)
    tgt_out[...] = flat_ref[...].astype(BF16).reshape(tgt_out.shape)
    quarter = tgt_out.shape[0] // 2
    mine = core * quarter
    last = mine + quarter - 1
    pl.semaphore_wait(barrier, len(greeted))
    hops = [send(tgt_out.at[mine + k], tgt_in.at[mine + k], k, ahead) for k in range(quarter)]
    direct = send(tgt_out.at[last], tgt_in.at[last], 2 * quarter - 1, across)
    target = relaid(flat_ref, z_ref, width)
    raw[1].wait()
    flattened(src_ref, flat_ref)
    source = relaid(flat_ref, z_ref, width)
    source_ref[...] = source
    for load in loads:
        load.wait()
    rows = source.shape[0] // n_wide

    def scatter(target, turn):
        pair = (source_ref[...] * target).astype(BF16)
        term = source_ref[...] * exchange(pair, tables, y_ref, grid, group)
        for k in range(n_wide):
            parts_out[turn, k] = term[k * rows : (k + 1) * rows].astype(BF16)
        slot = 2 * quarter + 1 + turn * (n_wide - 1)
        return [
            send(parts_out.at[turn, other], parts_in.at[turn, d], slot + d, (other, b))
            for other, d in peers
        ]

    def gathered(copies, turn):
        summed = parts_out[turn, w].astype(F32)
        for (_, d), copy in reversed(list(zip(peers, copies))):
            copy.wait()
            summed = summed + parts_in[turn, d].astype(F32)
        return summed

    first = scatter(target, 0)
    relays = []
    for k, hop in enumerate(hops):
        hop.wait()
        if k < quarter - 1:
            here = tgt_in.at[mine + k]
            relays.append(send(here, here, quarter + k, partner))
    for relay in relays:
        relay.wait()
    direct.wait()
    flat_ref[...] = tgt_in[...].astype(F32).reshape(flat_ref.shape)
    second = scatter(relaid(flat_ref, z_ref, width), 1)
    passed_out[...] = gathered(first, 0).astype(BF16)
    passed = send(passed_out, passed_in, 2 * quarter, ahead)
    summed = gathered(second, 1)
    passed.wait()
    summed = summed + passed_in[...].astype(F32)
    for k in range(rows):
        out_ref[0:1, k * width : (k + 1) * width] = summed[k : k + 1, :width]


def shards(n_wide, n_blk, sources, targets):
    cells = sources.shape[1]
    grid = round(cells ** (1.0 / 3.0))
    group, tables = plan(grid)
    wide = 2 * LANES
    rows = cells // (group * grid)
    part = rows // n_wide
    line = 8 * -(-cells // (64 * LANES))
    vmem = pl.BlockSpec(memory_space=pltpu.VMEM)
    hbm = pl.BlockSpec(memory_space=pltpu.HBM)
    sems = 8 + 1 + 2 * (n_wide - 1)
    result = pl.pallas_call(
        functools.partial(kernel, n_wide, n_blk, grid, group),
        out_shape=pltpu.VMEM((1, cells // n_wide), F32),
        in_specs=[hbm] * 9,
        out_specs=vmem,
        scratch_shapes=[pltpu.VMEM(t.shape, t.dtype) for t in tables]
        + [
            pltpu.VMEM((1, cells), BF16),
            pltpu.VMEM((1, cells), BF16),
            pltpu.VMEM((rows // 2 * group, LANES), F32),
            pltpu.VMEM((8 * line, LANES), F32),
            pltpu.VMEM((2, rows, LANES), F32),
            pltpu.VMEM((rows, wide), F32),
            pltpu.VMEM((8, line, LANES), BF16),
            pltpu.VMEM((8, line, LANES), BF16),
            pltpu.VMEM((2, n_wide, part, wide), BF16),
            pltpu.VMEM((2, n_wide - 1, part, wide), BF16),
            pltpu.VMEM((part, wide), BF16),
            pltpu.VMEM((part, wide), BF16),
            pltpu.SemaphoreType.DMA((2,)),
            pltpu.SemaphoreType.DMA((len(tables),)),
            pltpu.SemaphoreType.DMA((sems,)),
            pltpu.SemaphoreType.DMA((sems,)),
        ],
        compiler_params=pltpu.CompilerParams(collective_id=0, has_side_effects=True, vmem_limit_bytes=56 << 20),
    )(sources, targets, *[jnp.asarray(t) for t in tables])
    return -result


def solution(mesh):
    body = functools.partial(shards, mesh.shape["wide"], mesh.shape["blk"])
    in_specs = (P(("wide", "blk"), None), P("blk", None))
    return jax.shard_map(
        body, mesh=mesh, in_specs=in_specs, out_specs=P("blk", "wide"), check_vma=False
    )
```
